32 devices in a mesh: dp: 4 (over z), tensor: 2 (over x), expert: 4 (over y, core).
Axes of the slice: x: 2, y: 2, z: 4, core: 2. Of those that a mesh axis runs over, the one named last changes fastest.
Arguments:
- block_in: bfloat16 [4096, 2048], P(('dp', 'expert'), 'tensor')
- route_ids: int32 [4096, 8], P(('dp', 'expert')), may hold values from 0 to 31, as said below
- route_weights: float32 [4096, 8], P(('dp', 'expert')), may hold values from 0.04 to 0.3
- cotangent: bfloat16 [4096, 2048], P(('dp', 'expert'), 'tensor'), may hold values from -6 to 6
- attention_gain: bfloat16 [2048], P('dp'), may hold values from 0.5 to 1.5
- query_weight: bfloat16 [2048, 4096], P('dp', 'tensor'), may hold values from -0.125 to 0.125
- key_projection_matrix: bfloat16 [2048, 512], P('dp', 'tensor'), may hold values from -0.125 to 0.125
- value_projection_matrix: bfloat16 [2048, 512], P('dp', 'tensor'), may hold values from -0.125 to 0.125
- output_weight: bfloat16 [2048, 4096], P('dp', 'tensor'), may hold values from -0.75 to 0.75
- query_gain: bfloat16 [128], P('dp'), may hold values from 0.5 to 1.5
- key_gain: bfloat16 [128], P('dp'), may hold values from 0.5 to 1.5
- expert_gain: bfloat16 [2048], P('dp'), may hold values from 0.5 to 1.5
- expert_gate_matrix: bfloat16 [32, 2048, 768], P(('dp', 'expert'), None, 'tensor'), may hold values from -0.125 to 0.125
- expert_up_matrix: bfloat16 [32, 2048, 768], P(('dp', 'expert'), None, 'tensor'), may hold values from -0.125 to 0.125
- expert_down_matrix: bfloat16 [32, 768, 2048], P(('dp', 'expert'), 'tensor'), may hold values from -0.625 to 0.625
Outputs:
- block_out: bfloat16 [4096, 2048], P(('dp', 'expert'), 'tensor')
- block_in_grad: float32 [4096, 2048], P(('dp', 'expert'), 'tensor')
- attention_gain_grad: float32 [2048], P('dp')
- query_weight_grad: float32 [2048, 4096], P('dp', 'tensor')
- key_weight_grad: float32 [2048, 512], P('dp', 'tensor')
- value_weight_grad: float32 [2048, 512], P('dp', 'tensor')
- output_weight_grad: float32 [2048, 4096], P('dp', 'tensor')
- query_gain_grad: float32 [128], P('dp')
- key_gain_grad: float32 [128], P('dp')
- expert_gain_grad: float32 [2048], P('dp')
- gate_grad: float32 [32, 2048, 768], P(('dp', 'expert'), None, 'tensor')
- up_matrix_gradient: float32 [32, 2048, 768], P(('dp', 'expert'), None, 'tensor')
- down_grad: float32 [32, 768, 2048], P(('dp', 'expert'), 'tensor')
The draws below stay inside these ranges and needn't reach their ends.
Inputs may be any that keep to these rules, and one draw needn't show every extreme that they name: `route_ids`: each row names 8 different experts. Among the 256 rows of one device (aligned blocks of rows), no expert is named by more than 128 rows, and in every draw some expert is named by exactly 128 rows in every block.
All inputs are finite; a program needn't handle non-finite values.
Results may differ from the reference program's by a relative error of at most 0.025.
Values may be sent and summed in bfloat16 or wider, within the bound.
No kernel may reach another device: no remote copies, remote signals or barrier semaphores. Data moves between devices by JAX's collectives and lax.ppermute only.
A program may use at most 384 MiB of HBM per device.

```python
import math
import jax
import jax.numpy as jnp
from jax import lax

MODEL_WIDTH = 2048
HQ = 32
KEY_VALUE_HEADS = 4
HEAD_SIZE = 128
FF = 768
TOPK = 8
E = 32
TOK_DEV = 256
SEQ = 256
TOKENS = 4096
CAP = 128
N_TENSOR = 2


def draw_block_in(key, part):
    first_key = jax.random.fold_in(jax.random.fold_in(key, 7), 0)
    normal_part = jnp.clip(jax.random.normal(first_key, (TOKENS, MODEL_WIDTH), jnp.float32), -5.0, 5.0)
    return normal_part.astype(jnp.bfloat16)


def draw_route_ids(key, part):
    groups = E // TOPK
    order_key, rank_key = jax.random.split(jax.random.fold_in(key, 11))
    expert_order = jax.random.permutation(order_key, E).astype(jnp.int32)
    block_total = TOKENS // TOK_DEV
    rank_keys = jax.random.split(rank_key, block_total * TOPK)
    rank_rows = jax.vmap(lambda single: jax.random.permutation(single, TOK_DEV))(rank_keys).astype(jnp.int32)
    rank_rows = rank_rows.reshape(block_total, TOPK, TOK_DEV)
    remaining = max(TOK_DEV - CAP, 1)
    local_index = jnp.where(rank_rows < CAP, 0, 1 + (groups - 1) * (rank_rows - CAP) // remaining)
    group_start = jnp.arange(TOPK, dtype=jnp.int32)[None, :, None] * groups
    chosen = jnp.take(expert_order, group_start + local_index)
    return jnp.transpose(chosen, (0, 2, 1)).reshape(TOKENS, TOPK).astype(jnp.int32)


def steps_of(stream_key, shape, cuts, least, top_value):
    gain, own = 1.0, jax.random.fold_in(stream_key, 6)
    for axis_at, parts in cuts:
        heights = jnp.exp(jax.random.uniform(jax.random.fold_in(own, axis_at), (parts,), jnp.float32, least / len(cuts), top_value / len(cuts)))
        gain = gain * jnp.repeat(heights, shape[axis_at] // parts).reshape([-1 if axis == axis_at else 1 for axis in range(len(shape))])
    return gain


def gaussian(stream_key, dims, scale, bound, cuts=(), held_as=jnp.bfloat16):
    drawn = jax.random.normal(stream_key, dims, jnp.float32) * scale
    if len(cuts) > 0:
        drawn = steps_of(stream_key, dims, cuts, -0.22, 0.18) * drawn
    return jnp.clip(drawn, min=-bound, max=bound).astype(held_as)


def setup_inputs(seed: int = 0) -> dict:
    key_of = jax.random.split(jax.random.key(seed), 16)
    block_in = draw_block_in(jax.random.fold_in(key_of[15], 71), 0)
    route_ids = draw_route_ids(jax.random.fold_in(key_of[15], 71), 0)
    route_weights = jnp.clip(jnp.exp(math.log(0.3) - 2.014903 * jax.random.uniform(key_of[2], (TOKENS, TOPK), jnp.float32) ** steps_of(key_of[2], (TOKENS, TOPK), ((0, 16),), -0.2, 0.2)), 0.04, 0.3)
    cotangent = gaussian(key_of[3], (TOKENS, MODEL_WIDTH), 1.0, 6.0, ((0, 16), (1, 2)))
    attention_gain = jnp.clip(1.0 + 0.1 * jax.random.normal(key_of[4], (MODEL_WIDTH,), jnp.float32), 0.5, 1.5).astype(jnp.bfloat16)
    query_weight = gaussian(key_of[5], (MODEL_WIDTH, HQ * HEAD_SIZE), MODEL_WIDTH ** -0.5, 0.125, ((0, 4), (1, 2)))
    key_projection_matrix = gaussian(key_of[6], (MODEL_WIDTH, KEY_VALUE_HEADS * HEAD_SIZE), MODEL_WIDTH ** -0.5, 0.125, ((0, 4), (1, 2)))
    value_projection_matrix = gaussian(key_of[7], (MODEL_WIDTH, KEY_VALUE_HEADS * HEAD_SIZE), MODEL_WIDTH ** -0.5, 0.125, ((0, 4), (1, 2)))
    output_weight = gaussian(key_of[8], (MODEL_WIDTH, HQ * HEAD_SIZE), (HQ * HEAD_SIZE * 4 // SEQ) ** -0.5, 0.75, ((0, 4), (1, 2)))
    query_gain = jnp.clip(1.0 + 0.1 * jax.random.normal(key_of[9], (HEAD_SIZE,), jnp.float32), 0.5, 1.5).astype(jnp.bfloat16)
    key_gain = jnp.clip(1.0 + 0.1 * jax.random.normal(key_of[10], (HEAD_SIZE,), jnp.float32), 0.5, 1.5).astype(jnp.bfloat16)
    expert_gain = jnp.clip(1.0 + 0.1 * jax.random.normal(key_of[11], (MODEL_WIDTH,), jnp.float32), 0.5, 1.5).astype(jnp.bfloat16)
    expert_gate_matrix = gaussian(key_of[12], (E, MODEL_WIDTH, FF), MODEL_WIDTH ** -0.5, 0.125, ((0, 16), (2, 2)))
    expert_up_matrix = gaussian(key_of[13], (E, MODEL_WIDTH, FF), MODEL_WIDTH ** -0.5, 0.125, ((0, 16), (2, 2)))
    expert_down_matrix = gaussian(key_of[14], (E, FF, MODEL_WIDTH), (FF // 8) ** -0.5, 0.625, ((0, 16), (1, 2)))
    return {"block_in": block_in, "route_ids": route_ids, "route_weights": route_weights, "cotangent": cotangent, "attention_gain": attention_gain, "query_weight": query_weight, "key_projection_matrix": key_projection_matrix, "value_projection_matrix": value_projection_matrix, "output_weight": output_weight, "query_gain": query_gain, "key_gain": key_gain, "expert_gain": expert_gain, "expert_gate_matrix": expert_gate_matrix, "expert_up_matrix": expert_up_matrix, "expert_down_matrix": expert_down_matrix}


epsilon = 1e-06
rope_base = 1000000.0

def to_half(values):
    return lax.optimization_barrier(values.astype(jnp.bfloat16))

def rope_tables(positions):
    half_dim = HEAD_SIZE // 2
    frequency = rope_base ** (-(jnp.arange(half_dim, dtype=jnp.float32) * 2.0) / HEAD_SIZE)
    angles = positions.astype(jnp.float32)[:, None] * frequency[None, :]
    angles = jnp.concatenate([angles, angles], axis=1)
    return (jnp.cos(angles)[:, None, :], jnp.sin(angles)[:, None, :])

def prepare(values, scales, cosine, sine_table, factor):
    mean_sq = lax.optimization_barrier(jnp.mean(values * values, axis=-1, keepdims=True))
    normed = values * lax.rsqrt(mean_sq + epsilon) * scales
    half_dim = values.shape[-1] // 2
    turned = jnp.concatenate([-normed[..., half_dim:], normed[..., :half_dim]], axis=-1)
    return (normed * cosine + turned * sine_table) * factor

def dot_last(first_arr, second_arr):
    return lax.dot_general(first_arr, second_arr, (((1,), (1,)), ((), ())), preferred_element_type=jnp.float32)

def dot_first(first_arr, second_arr):
    return lax.dot_general(first_arr, second_arr, (((0,), (0,)), ((), ())), preferred_element_type=jnp.float32)

def forward_rows(block_rows, norm_first, query_weight, key_projection_matrix, value_projection_matrix, query_scale, key_scale, cosine, sine_table, causal):
    row_count = block_rows.shape[0]
    input_float = block_rows.astype(jnp.float32)
    inv_first = lax.rsqrt(lax.optimization_barrier(jnp.mean(input_float * input_float, axis=1, keepdims=True)) + epsilon)
    input_hat = input_float * inv_first
    normed = to_half(input_hat * norm_first)
    queries = jnp.dot(normed, query_weight, preferred_element_type=jnp.float32).reshape(row_count, -1, HEAD_SIZE)
    key_rows = jnp.dot(normed, key_projection_matrix, preferred_element_type=jnp.float32).reshape(row_count, -1, HEAD_SIZE)
    value_rows = to_half(jnp.dot(normed, value_projection_matrix, preferred_element_type=jnp.float32))
    key_heads = key_rows.shape[1]
    group_size = queries.shape[1] // key_heads
    seq_count = row_count // SEQ
    query_rot = to_half(prepare(queries, query_scale, cosine, sine_table, 1.0 / math.sqrt(HEAD_SIZE)))
    key_rot = to_half(prepare(key_rows, key_scale, cosine, sine_table, 1.0))
    query_seq = query_rot.reshape(seq_count, SEQ, key_heads, group_size, HEAD_SIZE)
    key_seq = key_rot.reshape(seq_count, SEQ, key_heads, HEAD_SIZE)
    value_seq = value_rows.reshape(seq_count, SEQ, key_heads, HEAD_SIZE)
    scores = jnp.einsum('nqhgd,nkhd->nhgqk', query_seq.astype(jnp.float32), key_seq.astype(jnp.float32))
    log_total = jnp.log(lax.optimization_barrier(jnp.sum(jnp.where(causal, jnp.exp(scores), 0.0), axis=-1)))
    soft_weights = jnp.where(causal, jnp.exp(scores - log_total[..., None]), 0.0)
    prob_half = to_half(soft_weights)
    attended = to_half(jnp.einsum('nhgqk,nkhd->nqhgd', prob_half.astype(jnp.float32), value_seq.astype(jnp.float32))).reshape(row_count, -1)
    return (input_float, inv_first, input_hat, normed, queries, key_rows, query_seq, key_seq, value_seq, soft_weights, prob_half, attended)

def reference(block_in, route_ids, route_weights, cotangent, attention_gain, query_weight, key_projection_matrix, value_projection_matrix, output_weight, query_gain, key_gain, expert_gain, expert_gate_matrix, expert_up_matrix, expert_down_matrix):
    block_count = TOKENS // TOK_DEV
    model_width = block_in.shape[1]
    positions = jnp.arange(TOK_DEV, dtype=jnp.int32) % SEQ
    cosine, sine_table = rope_tables(positions)
    causal = jnp.arange(SEQ)[None, :] <= jnp.arange(SEQ)[:, None]
    factor = 1.0 / math.sqrt(HEAD_SIZE)
    norm_first = attention_gain.astype(jnp.float32)
    query_scale = query_gain.astype(jnp.float32)
    key_scale = key_gain.astype(jnp.float32)
    norm_second = expert_gain.astype(jnp.float32)
    input_blocks = block_in.reshape(block_count, TOK_DEV, model_width)

    def residual_rows(block_rows):
        pieces = forward_rows(block_rows, norm_first, query_weight, key_projection_matrix, value_projection_matrix, query_scale, key_scale, cosine, sine_table, causal)
        return pieces[0] + dot_last(pieces[11], output_weight)
    residual = lax.map(residual_rows, input_blocks).reshape(TOKENS, model_width)
    inv_second = lax.rsqrt(lax.optimization_barrier(jnp.mean(residual * residual, axis=1, keepdims=True)) + epsilon)
    resid_hat = residual * inv_second
    expert_in = to_half(resid_hat * norm_second)
    hit_counts = lax.optimization_barrier(jnp.sum((route_ids[:, :, None] == jnp.arange(E, dtype=jnp.int32)[None, None, :]).astype(jnp.int32), axis=1))
    hit_counts = hit_counts.reshape(block_count, TOK_DEV, E)
    earlier = (jnp.cumsum(hit_counts, axis=1) - hit_counts).reshape(TOKENS, E)
    position = jnp.take_along_axis(earlier, route_ids, axis=1)
    block_of = (jnp.arange(TOKENS, dtype=jnp.int32) // TOK_DEV)[:, None]
    slot_index = route_ids * (block_count * CAP) + block_of * CAP + position
    entry_count = TOKENS * TOPK
    slot_table = jnp.full((E * block_count * CAP,), entry_count, jnp.int32)
    slot_table = slot_table.at[slot_index.reshape(-1)].set(jnp.arange(entry_count, dtype=jnp.int32))
    slot_table = slot_table.reshape(E, block_count * CAP)
    expert_pad = jnp.concatenate([expert_in, jnp.zeros((1, model_width), jnp.bfloat16)], axis=0)
    weight_pad = jnp.concatenate([route_weights.reshape(-1), jnp.zeros((1,), jnp.float32)])
    grad_float = cotangent.astype(jnp.float32)
    grad_pad = jnp.concatenate([grad_float, jnp.zeros((1, model_width), jnp.float32)], axis=0)
    piece_width = FF // N_TENSOR

    def expert_forward(running, inputs):
        entries, gate_mat, up_mat, down_mat = inputs
        token_rows = entries // TOPK
        slot_rows = jnp.take(expert_pad, token_rows, axis=0)
        slot_weight = jnp.take(weight_pad, entries)
        gate_pre = jnp.dot(slot_rows, gate_mat, preferred_element_type=jnp.float32)
        up_projected = jnp.dot(slot_rows, up_mat, preferred_element_type=jnp.float32)
        sigmoid = jax.nn.sigmoid(gate_pre)
        swish_product = to_half(gate_pre * sigmoid * up_projected)
        summed = jnp.zeros((slot_rows.shape[0], model_width), jnp.float32)
        for segment in range(N_TENSOR):
            low_col = segment * piece_width
            produced = to_half(jnp.dot(swish_product[:, low_col:low_col + piece_width], down_mat[low_col:low_col + piece_width], preferred_element_type=jnp.float32))
            summed = summed + produced.astype(jnp.float32)
        running = running.at[token_rows].add(slot_weight[:, None] * summed)
        return (running, None)
    mixture, _ = lax.scan(expert_forward, jnp.zeros((TOKENS + 1, model_width), jnp.float32), (slot_table, expert_gate_matrix, expert_up_matrix, expert_down_matrix))
    block_out = (residual + mixture[:TOKENS]).astype(jnp.bfloat16)

    def expert_backward(running, inputs):
        entries, gate_mat, up_mat, down_mat = inputs
        token_rows = entries // TOPK
        slot_rows = jnp.take(expert_pad, token_rows, axis=0)
        slot_weight = jnp.take(weight_pad, entries)
        slot_grad = to_half(slot_weight[:, None] * jnp.take(grad_pad, token_rows, axis=0))
        gate_pre = jnp.dot(slot_rows, gate_mat, preferred_element_type=jnp.float32)
        up_projected = jnp.dot(slot_rows, up_mat, preferred_element_type=jnp.float32)
        sigmoid = jax.nn.sigmoid(gate_pre)
        swish_act = gate_pre * sigmoid
        swish_product = to_half(swish_act * up_projected)
        act_grad = dot_last(slot_grad, down_mat)
        gate_pre_gradient = to_half(act_grad * up_projected * sigmoid * (1.0 + gate_pre * (1.0 - sigmoid)))
        up_pre_gradient = to_half(act_grad * swish_act)
        down_part = dot_first(swish_product, slot_grad)
        gate_part = dot_first(slot_rows, gate_pre_gradient)
        up_part = dot_first(slot_rows, up_pre_gradient)
        summed = jnp.zeros((slot_rows.shape[0], model_width), jnp.float32)
        for segment in range(N_TENSOR):
            low_col = segment * piece_width
            high_col = low_col + piece_width
            produced = to_half(dot_last(gate_pre_gradient[:, low_col:high_col], gate_mat[:, low_col:high_col]) + dot_last(up_pre_gradient[:, low_col:high_col], up_mat[:, low_col:high_col]))
            summed = summed + produced.astype(jnp.float32)
        running = running.at[token_rows].add(summed)
        return (running, (gate_part, up_part, down_part))
    expert_back, (gate_grad, up_matrix_gradient, down_grad) = lax.scan(expert_backward, jnp.zeros((TOKENS + 1, model_width), jnp.float32), (slot_table, expert_gate_matrix, expert_up_matrix, expert_down_matrix))
    expert_in_grad = expert_back[:TOKENS]
    scaled = expert_in_grad * norm_second
    resid_grad = grad_float + inv_second * (scaled - resid_hat * lax.optimization_barrier(jnp.mean(scaled * resid_hat, axis=1, keepdims=True)))
    expert_gain_grad = lax.optimization_barrier(jnp.sum(expert_in_grad * resid_hat, axis=0))

    def attend_backward(running, inputs):
        block_rows, grad_rows = inputs
        input_float, inv_first, input_hat, normed, queries, key_rows, query_seq, key_seq, value_seq, soft_weights, prob_half, attended = forward_rows(block_rows, norm_first, query_weight, key_projection_matrix, value_projection_matrix, query_scale, key_scale, cosine, sine_table, causal)
        row_count = block_rows.shape[0]
        resid_cast = to_half(grad_rows)
        attended_grad = to_half(jnp.dot(resid_cast, output_weight, preferred_element_type=jnp.float32))
        output_part = dot_first(resid_cast, attended)
        grad_seq = attended_grad.reshape(query_seq.shape)
        value_grad = to_half(jnp.einsum('nhgqk,nqhgd->nkhd', prob_half.astype(jnp.float32), grad_seq.astype(jnp.float32))).reshape(row_count, -1)
        prob_grad = jnp.einsum('nqhgd,nkhd->nhgqk', grad_seq.astype(jnp.float32), value_seq.astype(jnp.float32))
        row_inner = lax.optimization_barrier(jnp.sum(soft_weights * prob_grad, axis=-1, keepdims=True))
        score_grad = to_half(soft_weights * (prob_grad - row_inner))
        query_rot_grad = jnp.einsum('nhgqk,nkhd->nqhgd', score_grad.astype(jnp.float32), key_seq.astype(jnp.float32)).reshape(queries.shape)
        key_rot_grad = jnp.einsum('nhgqk,nqhgd->nkhd', score_grad.astype(jnp.float32), query_seq.astype(jnp.float32)).reshape(key_rows.shape)
        _, query_pull = jax.vjp(lambda values, scales: prepare(values, scales, cosine, sine_table, factor), queries, query_scale)
        query_grad, query_scale_grad = query_pull(query_rot_grad)
        _, key_pull = jax.vjp(lambda values, scales: prepare(values, scales, cosine, sine_table, 1.0), key_rows, key_scale)
        key_grad, key_scale_grad = key_pull(key_rot_grad)
        query_cast = to_half(query_grad.reshape(row_count, -1))
        key_cast = to_half(key_grad.reshape(row_count, -1))
        normed_grad = dot_last(query_cast, query_weight) + dot_last(key_cast, key_projection_matrix) + dot_last(value_grad, value_projection_matrix)
        scaled_first = normed_grad * norm_first
        input_grad = grad_rows + inv_first * (scaled_first - input_hat * lax.optimization_barrier(jnp.mean(scaled_first * input_hat, axis=1, keepdims=True)))
        updates = (dot_first(normed, query_cast), dot_first(normed, key_cast), dot_first(normed, value_grad), output_part, lax.optimization_barrier(jnp.sum(normed_grad * input_hat, axis=0)), query_scale_grad, key_scale_grad)
        running = jax.tree.map(jnp.add, running, updates)
        return (running, input_grad)
    zero_init = (jnp.zeros(query_weight.shape, jnp.float32), jnp.zeros(key_projection_matrix.shape, jnp.float32), jnp.zeros(value_projection_matrix.shape, jnp.float32), jnp.zeros(output_weight.shape, jnp.float32), jnp.zeros((model_width,), jnp.float32), jnp.zeros((HEAD_SIZE,), jnp.float32), jnp.zeros((HEAD_SIZE,), jnp.float32))
    totals, input_grads = lax.scan(attend_backward, zero_init, (input_blocks, resid_grad.reshape(block_count, TOK_DEV, model_width)))
    block_in_grad = input_grads.reshape(TOKENS, model_width)
    return (block_out, block_in_grad, totals[4], totals[0], totals[1], totals[2], totals[3], totals[5], totals[6], expert_gain_grad, gate_grad, up_matrix_gradient, down_grad)
```

```python
import math

import jax
import jax.numpy as jnp
from jax import lax
from jax.sharding import PartitionSpec as P

HEAD_SIZE = 128
SEQ = 256
CHUNK_TOKENS = 4096
ROWS = ("dp", "expert")
WHOLE = ("tensor", "dp", "expert")

epsilon = 1e-06
rope_base = 1000000.0


def rope_tables(positions):
    half_dim = HEAD_SIZE // 2
    frequency = rope_base ** (-(jnp.arange(half_dim, dtype=jnp.float32) * 2.0) / HEAD_SIZE)
    angles = positions.astype(jnp.float32)[:, None] * frequency[None, :]
    angles = jnp.concatenate([angles, angles], axis=1)
    return (jnp.cos(angles)[:, None, :], jnp.sin(angles)[:, None, :])


def prepare(values, scales, cosine, sine_table, factor):
    mean_sq = jnp.mean(values * values, axis=-1, keepdims=True)
    normed = values * lax.rsqrt(mean_sq + epsilon) * scales
    half_dim = values.shape[-1] // 2
    turned = jnp.concatenate([-normed[..., half_dim:], normed[..., :half_dim]], axis=-1)
    return (normed * cosine + turned * sine_table) * factor


def dot(first_arr, second_arr):
    return jnp.dot(first_arr, second_arr, preferred_element_type=jnp.float32)


def dot_last(first_arr, second_arr):
    return lax.dot_general(
        first_arr, second_arr, (((1,), (1,)), ((), ())), preferred_element_type=jnp.float32
    )


def dot_first(first_arr, second_arr):
    return lax.dot_general(
        first_arr, second_arr, (((0,), (0,)), ((), ())), preferred_element_type=jnp.float32
    )


def own_rows(weight):
    rows = weight.shape[0] // lax.axis_size("expert")
    return lax.dynamic_slice_in_dim(weight, lax.axis_index("expert") * rows, rows, 0)


def gather_weight(weight):
    return lax.all_gather(weight, ROWS, axis=0, tiled=True)


def scatter_weight(gradient):
    piece = lax.psum_scatter(gradient.astype(jnp.bfloat16), ROWS, scatter_dimension=0, tiled=True)
    return lax.all_gather(piece, "expert", axis=0, tiled=True).astype(jnp.float32)


def local(
    block_in,
    route_ids,
    route_weights,
    cotangent,
    attention_gain,
    query_weight,
    key_projection_matrix,
    value_projection_matrix,
    output_weight,
    query_gain,
    key_gain,
    expert_gain,
    expert_gate_matrix,
    expert_up_matrix,
    expert_down_matrix,
):
    row_count, half_width = block_in.shape
    halves = lax.axis_size("tensor")
    model_width = half_width * halves
    group_devices = lax.axis_size(ROWS)
    local_experts = expert_gate_matrix.shape[0]
    expert_total = local_experts * group_devices
    hidden = expert_gate_matrix.shape[2]
    offset = lax.axis_index("tensor") * half_width
    group_index = lax.axis_index(ROWS)

    expert_names = jnp.arange(expert_total, dtype=jnp.int32)
    dense = jnp.sum(
        jnp.where(
            route_ids[:, :, None] == expert_names[None, None, :], route_weights[:, :, None], 0.0
        ),
        axis=1,
    ).T
    gains = jnp.concatenate([attention_gain, expert_gain, query_gain, key_gain]).astype(jnp.float32)
    table = jnp.concatenate([dense.reshape(-1), gains])
    table = lax.all_gather(table, ROWS, axis=0, tiled=False)
    full_in = lax.all_gather(block_in, "tensor", axis=1, tiled=True)

    qkv_full = gather_weight(
        jnp.concatenate(
            [
                own_rows(query_weight),
                own_rows(key_projection_matrix),
                own_rows(value_projection_matrix),
            ],
            axis=1,
        )
    )
    output_full = gather_weight(own_rows(output_weight))

    routed = table[:, : expert_total * row_count].reshape(group_devices, expert_total, row_count)
    routed = lax.dynamic_slice_in_dim(routed, group_index * local_experts, local_experts, 1)
    gain_rows = table[:, expert_total * row_count :].reshape(
        lax.axis_size("dp"), lax.axis_size("expert"), -1
    )[:, 0]
    width_rows = attention_gain.shape[0]
    head_rows = query_gain.shape[0]
    norm_first = gain_rows[:, :width_rows].reshape(-1)
    norm_second = gain_rows[:, width_rows : 2 * width_rows].reshape(-1)
    query_scale = gain_rows[:, 2 * width_rows : 2 * width_rows + head_rows].reshape(-1)
    key_scale = gain_rows[:, 2 * width_rows + head_rows :].reshape(-1)
    first_half = lax.dynamic_slice_in_dim(norm_first, offset, half_width, 0)
    second_half = lax.dynamic_slice_in_dim(norm_second, offset, half_width, 0)

    input_float = full_in.astype(jnp.float32)
    inv_first = lax.rsqrt(jnp.mean(input_float * input_float, axis=1, keepdims=True) + epsilon)
    normed = (input_float * inv_first * norm_first).astype(jnp.bfloat16)
    block_float = block_in.astype(jnp.float32)
    input_hat = block_float * inv_first
    query_cols = query_weight.shape[1]
    key_cols = key_projection_matrix.shape[1]
    heads_local = query_cols // HEAD_SIZE
    key_heads = key_cols // HEAD_SIZE
    group_size = heads_local // key_heads
    seq_count = row_count // SEQ
    projected = dot(normed, qkv_full)
    queries = projected[:, :query_cols].reshape(row_count, heads_local, HEAD_SIZE)
    key_rows = projected[:, query_cols : query_cols + key_cols].reshape(
        row_count, key_heads, HEAD_SIZE
    )
    value_rows = projected[:, query_cols + key_cols :].astype(jnp.bfloat16)
    positions = jnp.arange(row_count, dtype=jnp.int32) % SEQ
    cosine, sine_table = rope_tables(positions)
    factor = 1.0 / math.sqrt(HEAD_SIZE)
    query_rot = prepare(queries, query_scale, cosine, sine_table, factor).astype(jnp.bfloat16)
    key_rot = prepare(key_rows, key_scale, cosine, sine_table, 1.0).astype(jnp.bfloat16)
    query_seq = query_rot.reshape(seq_count, SEQ, key_heads, group_size, HEAD_SIZE)
    key_seq = key_rot.reshape(seq_count, SEQ, key_heads, HEAD_SIZE)
    value_seq = value_rows.reshape(seq_count, SEQ, key_heads, HEAD_SIZE)
    causal = jnp.arange(SEQ)[None, :] <= jnp.arange(SEQ)[:, None]
    scores = jnp.einsum("nqhgd,nkhd->nhgqk", query_seq, key_seq, preferred_element_type=jnp.float32)
    log_total = jnp.log(jnp.sum(jnp.where(causal, jnp.exp(scores), 0.0), axis=-1))
    soft_weights = jnp.where(causal, jnp.exp(scores - log_total[..., None]), 0.0)
    prob_half = soft_weights.astype(jnp.bfloat16)
    attended = (
        jnp.einsum("nhgqk,nkhd->nqhgd", prob_half, value_seq, preferred_element_type=jnp.float32)
        .astype(jnp.bfloat16)
        .reshape(row_count, heads_local * HEAD_SIZE)
    )
    head_total = lax.psum_scatter(
        dot_last(attended, output_full), "tensor", scatter_dimension=1, tiled=True
    )
    residual = block_float + head_total
    square_sum = lax.psum(jnp.sum(residual * residual, axis=1), "tensor")[:, None]
    inv_second = lax.rsqrt(square_sum / model_width + epsilon)
    resid_hat = residual * inv_second
    expert_in = (resid_hat * second_half).astype(jnp.bfloat16)

    first_layer = jnp.concatenate(
        [expert_gate_matrix[index] for index in range(local_experts)]
        + [expert_up_matrix[index] for index in range(local_experts)],
        axis=1,
    ).reshape(halves, half_width, 2 * local_experts * hidden)
    down = expert_down_matrix.reshape(local_experts * hidden, halves, half_width)
    down_halves = [down[:, index] for index in range(halves)]
    hidden_all = local_experts * hidden

    chunk_count = max(1, group_devices * row_count // CHUNK_TOKENS)
    chunk_rows = row_count // chunk_count
    chunk_total = chunk_rows * group_devices

    def everywhere(rows):
        gathered = lax.all_gather(rows, WHOLE, axis=0, tiled=True)
        return gathered.reshape(halves, chunk_total, half_width)

    mixture_parts, expert_back_parts = [], []
    down_grad = gate_grad = up_matrix_gradient = 0.0
    for chunk in range(chunk_count):
        low = chunk * chunk_rows
        rows_in = everywhere(expert_in[low : low + chunk_rows])
        rows_cot = everywhere(cotangent[low : low + chunk_rows])
        weight_cols = jnp.repeat(
            routed[:, :, low : low + chunk_rows]
            .transpose(0, 2, 1)
            .reshape(chunk_total, local_experts),
            hidden,
            axis=1,
        )
        hidden_pre = sum(dot(rows_in[index], first_layer[index]) for index in range(halves))
        gate_pre = hidden_pre[:, :hidden_all]
        up_pre = hidden_pre[:, hidden_all:]
        sigmoid = jax.nn.sigmoid(gate_pre)
        swish = gate_pre * sigmoid
        weighted = (swish * up_pre * weight_cols).astype(jnp.bfloat16)
        mixed = jnp.stack([dot(weighted, piece) for piece in down_halves])
        mixture_parts.append(
            lax.psum_scatter(
                mixed.astype(jnp.bfloat16).reshape(halves * chunk_total, half_width),
                WHOLE,
                scatter_dimension=0,
                tiled=True,
            )
        )
        act_grad = weight_cols * sum(
            dot_last(rows_cot[index], down_halves[index]) for index in range(halves)
        )
        gate_back = (act_grad * up_pre * sigmoid * (1.0 + gate_pre * (1.0 - sigmoid))).astype(
            jnp.bfloat16
        )
        up_back = (act_grad * swish).astype(jnp.bfloat16)
        both_back = jnp.concatenate([gate_back, up_back], axis=1)
        back = jnp.stack([dot_last(both_back, first_layer[index]) for index in range(halves)])
        expert_back_parts.append(
            lax.psum_scatter(
                back.astype(jnp.bfloat16).reshape(halves * chunk_total, half_width),
                WHOLE,
                scatter_dimension=0,
                tiled=True,
            )
        )
        down_grad = down_grad + jnp.concatenate(
            [dot_first(weighted, rows_cot[index]) for index in range(halves)], axis=1
        ).reshape(local_experts, hidden, model_width)
        gate_grad = gate_grad + jnp.stack(
            [
                jnp.concatenate(
                    [
                        dot_first(rows_in[index], gate_back[:, e * hidden : (e + 1) * hidden])
                        for index in range(halves)
                    ]
                )
                for e in range(local_experts)
            ]
        )
        up_matrix_gradient = up_matrix_gradient + jnp.stack(
            [
                jnp.concatenate(
                    [
                        dot_first(rows_in[index], up_back[:, e * hidden : (e + 1) * hidden])
                        for index in range(halves)
                    ]
                )
                for e in range(local_experts)
            ]
        )
    mixture = jnp.concatenate(mixture_parts).astype(jnp.float32)
    block_out = (residual + mixture).astype(jnp.bfloat16)
    expert_in_grad = jnp.concatenate(expert_back_parts).astype(jnp.float32)

    grad_float = cotangent.astype(jnp.float32)
    scaled = expert_in_grad * second_half
    back_mean = lax.psum(jnp.sum(scaled * resid_hat, axis=1), "tensor")[:, None] / model_width
    resid_grad = grad_float + inv_second * (scaled - resid_hat * back_mean)
    expert_gain_part = jnp.sum(expert_in_grad * resid_hat, axis=0)
    resid_cast = lax.all_gather(resid_grad.astype(jnp.bfloat16), "tensor", axis=1, tiled=True)
    output_weight_grad = scatter_weight(dot_first(resid_cast, attended))
    attended_grad = dot(resid_cast, output_full).astype(jnp.bfloat16)
    scores_again = jnp.einsum(
        "nqhgd,nkhd->nhgqk", query_seq, key_seq, preferred_element_type=jnp.float32
    )
    probs_again = jnp.where(causal, jnp.exp(scores_again - log_total[..., None]), 0.0)
    probs_again_half = probs_again.astype(jnp.bfloat16)
    grad_seq = attended_grad.reshape(seq_count, SEQ, key_heads, group_size, HEAD_SIZE)
    value_grad = (
        jnp.einsum(
            "nhgqk,nqhgd->nkhd", probs_again_half, grad_seq, preferred_element_type=jnp.float32
        )
        .astype(jnp.bfloat16)
        .reshape(row_count, key_heads * HEAD_SIZE)
    )
    prob_grad = jnp.einsum(
        "nqhgd,nkhd->nhgqk", grad_seq, value_seq, preferred_element_type=jnp.float32
    )
    row_inner = jnp.sum(probs_again * prob_grad, axis=-1, keepdims=True)
    score_grad = (probs_again * (prob_grad - row_inner)).astype(jnp.bfloat16)
    query_rot_grad = jnp.einsum(
        "nhgqk,nkhd->nqhgd", score_grad, key_seq, preferred_element_type=jnp.float32
    ).reshape(row_count, heads_local, HEAD_SIZE)
    key_rot_grad = jnp.einsum(
        "nhgqk,nqhgd->nkhd", score_grad, query_seq, preferred_element_type=jnp.float32
    ).reshape(row_count, key_heads, HEAD_SIZE)
    _, query_pull = jax.vjp(
        lambda values, scales: prepare(values, scales, cosine, sine_table, factor),
        queries,
        query_scale,
    )
    query_grad, query_scale_grad = query_pull(query_rot_grad)
    _, key_pull = jax.vjp(
        lambda values, scales: prepare(values, scales, cosine, sine_table, 1.0), key_rows, key_scale
    )
    key_grad, key_scale_grad = key_pull(key_rot_grad)
    casts = jnp.concatenate(
        [
            query_grad.reshape(row_count, query_cols).astype(jnp.bfloat16),
            key_grad.reshape(row_count, key_cols).astype(jnp.bfloat16),
            value_grad,
        ],
        axis=1,
    )
    normed_grad = lax.psum_scatter(
        dot_last(casts, qkv_full).astype(jnp.bfloat16), "tensor", scatter_dimension=1, tiled=True
    ).astype(jnp.float32)
    qkv_grad = scatter_weight(dot_first(normed, casts))
    scaled_first = normed_grad * first_half
    first_mean = lax.psum(jnp.sum(scaled_first * input_hat, axis=1), "tensor")[:, None]
    block_in_grad = resid_grad + inv_first * (scaled_first - input_hat * first_mean / model_width)
    attention_gain_part = jnp.sum(normed_grad * input_hat, axis=0)

    wide = jnp.zeros((2, model_width), jnp.float32)
    wide = lax.dynamic_update_slice(
        wide, jnp.stack([attention_gain_part, expert_gain_part]), (0, offset)
    )
    small = jnp.concatenate([wide[0], wide[1], query_scale_grad, key_scale_grad])
    small = lax.psum(small, WHOLE)
    dp_index = lax.axis_index("dp")

    def owned(start, rows):
        return lax.dynamic_slice_in_dim(small, start + dp_index * rows, rows, 0)

    return (
        block_out,
        block_in_grad,
        owned(0, width_rows),
        qkv_grad[:, :query_cols],
        qkv_grad[:, query_cols : query_cols + key_cols],
        qkv_grad[:, query_cols + key_cols :],
        output_weight_grad,
        owned(2 * model_width, head_rows),
        owned(2 * model_width + HEAD_SIZE, head_rows),
        owned(model_width, width_rows),
        gate_grad,
        up_matrix_gradient,
        down_grad,
    )


def solution(mesh):
    rows = P(ROWS, "tensor")
    weight = P("dp", "tensor")
    expert_cols = P(ROWS, None, "tensor")
    expert_rows = P(ROWS, "tensor", None)
    gain = P("dp")
    placed = (rows, P(ROWS, None), P(ROWS, None), rows, gain) + (weight,) * 4 + (gain,) * 3
    return jax.shard_map(
        local,
        mesh=mesh,
        in_specs=placed + (expert_cols, expert_cols, expert_rows),
        out_specs=(rows, rows, gain)
        + (weight,) * 4
        + (gain,) * 3
        + (expert_cols, expert_cols, expert_rows),
        check_vma=False,
    )
```
